32 devices in a mesh: run: 4 (over z), px: 4 (over x, core), py: 2 (over y).
Axes of the slice: x: 2, y: 2, z: 4, core: 2. Of those that a mesh axis runs over, the one named last changes fastest.
Arguments:
- current_estimate: bfloat16 [8, 2, 256, 256, 256], P('run', None, 'px', 'py'), may hold values from -6 to 6
- observed_magnitude: float32 [256, 256, 256], P(('px', 'py')), as said below
- object_bounds: int32 [256, 256, 2], P('px', 'py'), may hold values from 0 to 256, as said below
- damping_ordinal: int32 [8], replicated, may hold values from 0 to 7
- retained_trials: int32 [4], replicated, may hold values from 0 to 7, as said below
Outputs:
- iterate_next: bfloat16 [8, 2, 256, 256, 256], P('run', None, 'px', 'py')
- iterate_final: bfloat16 [4, 2, 256, 256, 256], P('run', None, 'px', 'py')
- errors_first: float32 [8], P('run')
- errors_final: float32 [4], P('run')
The draws below stay inside these ranges and needn't reach their ends.
Inputs may be any that keep to these rules, and one draw needn't show every extreme that they name: `observed_magnitude`: nonnegative magnitudes. object_bounds[i, j, 0] < object_bounds[i, j, 1] for every line. `retained_trials`: 4 different runs; run 0 and run 8 - 1 are always among them.
All inputs are finite; a program needn't handle non-finite values.
Results may differ from the reference program's by a relative error of at most 0.023.
Values may be sent and summed in bfloat16 or wider, within the bound.
No kernel may reach another device: no remote copies, remote signals or barrier semaphores. Data moves between devices by JAX's collectives and lax.ppermute only.
A program may use at most 256 MiB of HBM per device.

```python
import math
import jax
import jax.numpy as jnp
from jax import lax

N = 256
RUNS = 8
SURV = 4


def draw_observed_magnitude(key, part):
    key_across, key_rough = jax.random.split(jax.random.fold_in(key, 11), 2)
    ramp_rank = jnp.arange(N, dtype=jnp.float32) / N
    ramp = 10.0 ** (ramp_rank - 0.5)
    across = jnp.exp(jax.random.uniform(key_across, (N,), jnp.float32, math.log(0.3), math.log(3.0)))
    roughness = jax.random.uniform(key_rough, (N, N, N), jnp.float32, 0.25, 1.75)
    extra_scale = jnp.ones((N,), jnp.float32)
    return ramp[:, None, None] * across[None, :, None] * extra_scale[None, None, :] * roughness


def draw_object_bounds(key, part):
    key_lower, key_upper = jax.random.split(jax.random.fold_in(key, 23))
    lower = jax.random.randint(key_lower, (N, N), 0, N // 4)
    upper = N - jax.random.randint(key_upper, (N, N), 0, N // 4)
    return jnp.stack([lower, upper], axis=-1).astype(jnp.int32)


def draw_retained_trials(key, part):
    key_middle, key_order = jax.random.split(jax.random.fold_in(key, 37))
    middle = jax.random.permutation(key_middle, RUNS - 2) + 1
    chosen_runs = jnp.concatenate([jnp.array([0, RUNS - 1], jnp.int32), middle[:SURV - 2].astype(jnp.int32)])
    ordering = jax.random.permutation(key_order, SURV)
    return chosen_runs[ordering].astype(jnp.int32)


def with_ends(values, own_key, smallest, largest):
    dims = values.shape
    spot = [jax.random.randint(jax.random.fold_in(own_key, axis), (), 0, dims[axis]) for axis in range(len(dims))]
    values = values.at[tuple(spot)].set(smallest)
    longest = dims.index(max(dims))
    spot[longest] = (spot[longest] + 1) % dims[longest]
    return values.at[tuple(spot)].set(largest)


def level_of(stream_key, dims, shards, least, top_value):
    gain = 1.0
    for axis_at, shards_of in shards:
        steps = jax.random.uniform(jax.random.fold_in(jax.random.fold_in(stream_key, 6), axis_at), (shards_of,), jnp.float32, least / len(shards), top_value / len(shards))
        gain = gain * jnp.repeat(jnp.exp(steps), dims[axis_at] // shards_of).reshape((-1,) + (1,) * (len(dims) - 1 - axis_at))
    return gain


def normal_values(own_key, shape, width, reach, pieces=(), kind=jnp.bfloat16):
    drawn = width * jax.random.normal(own_key, shape, jnp.float32)
    if pieces:
        drawn = drawn * level_of(own_key, shape, pieces, -0.22, 0.18)
    return jnp.clip(drawn, -reach, reach).astype(kind)


def setup_inputs(seed: int = 0) -> dict:
    key_of = jax.random.split(jax.random.key(seed), 6)
    return {
        "current_estimate": normal_values(key_of[0], (RUNS, 2, N, N, N), 1.0, 6.0, ((0, 4), (2, 4), (3, 2))),
        "observed_magnitude": draw_observed_magnitude(jax.random.fold_in(key_of[5], 71), 0),
        "object_bounds": draw_object_bounds(jax.random.fold_in(key_of[5], 71), 0),
        "damping_ordinal": with_ends(jax.random.randint(key_of[3], (RUNS,), 0, 8), jax.random.fold_in(key_of[3], 1), 0, 7).astype(jnp.int32),
        "retained_trials": draw_retained_trials(jax.random.fold_in(key_of[5], 71), 0),
    }


def fourier_table(length, direction):
    positions = jnp.arange(length, dtype=jnp.int32)
    angles = (positions[:, None] * positions[None, :] % length).astype(jnp.float32) * (2.0 * math.pi / length)
    normalise = 1.0 / math.sqrt(length)
    cosine = jnp.cos(angles) * normalise
    sine_part = jnp.sin(angles) * normalise
    upper_row = jnp.stack([cosine, direction * sine_part])
    bottom = jnp.stack([-direction * sine_part, cosine])
    return jnp.stack([upper_row, bottom]).astype(jnp.bfloat16)

def transform(field, table, which_axis):
    patterns = {0: 'inbc,ionk->okbc', 1: 'ianc,ionk->oakc', 2: 'iabn,ionk->oabk'}
    return jnp.einsum(patterns[which_axis], field.astype(jnp.float32), table.astype(jnp.float32))

def rounded(field):
    return lax.optimization_barrier(field.astype(jnp.bfloat16))

def relax_step(current, beta, measured, inside, forward_table, inverse_table):
    after_z = rounded(transform(current, forward_table, 2))
    after_x = rounded(transform(after_z, forward_table, 0))
    spectrum = transform(after_x, forward_table, 1)
    amplitude = jnp.sqrt(spectrum[0] * spectrum[0] + spectrum[1] * spectrum[1])
    misfit = jnp.sum((amplitude - measured) ** 2)
    scaling = measured / jnp.maximum(amplitude, 0.1)
    target = rounded(spectrum * scaling[None])
    back_y = rounded(transform(target, inverse_table, 1))
    back_x = rounded(transform(back_y, inverse_table, 0))
    projected = transform(back_x, inverse_table, 2)
    outside_value = beta * current.astype(jnp.float32) + (1.0 - 2.0 * beta) * projected
    updated = jnp.where(inside[None], projected, outside_value).astype(jnp.bfloat16)
    return (updated, misfit)

def reference(current_estimate, observed_magnitude, object_bounds, damping_ordinal, retained_trials):
    forward_table = fourier_table(N, -1.0)
    inverse_table = fourier_table(N, 1.0)
    measured = jnp.transpose(observed_magnitude, (2, 1, 0)).astype(jnp.float32)
    energy = jnp.sum(measured * measured)
    position = jnp.arange(N, dtype=jnp.int32)
    inside = (position[None, None, :] >= object_bounds[:, :, 0:1]) & (position[None, None, :] < object_bounds[:, :, 1:2])
    damping_levels = 0.5 + 0.05 * (damping_ordinal.astype(jnp.float32) + 1.0)
    updated_runs = []
    first_errors = []
    for team_rank in range(RUNS):
        updated, misfit = relax_step(current_estimate[team_rank], damping_levels[team_rank], measured, inside, forward_table, inverse_table)
        updated_runs.append(updated)
        first_errors.append(misfit / energy)
    iterate_next = jnp.stack(updated_runs)
    final_runs = []
    final_errors = []
    for team_rank in range(SURV):
        chosen_trial = retained_trials[team_rank]
        current = lax.dynamic_index_in_dim(iterate_next, chosen_trial, 0, keepdims=False)
        updated, misfit = relax_step(current, damping_levels[chosen_trial], measured, inside, forward_table, inverse_table)
        final_runs.append(updated)
        final_errors.append(misfit / energy)
    return (iterate_next, jnp.stack(final_runs), jnp.stack(first_errors), jnp.stack(final_errors))
```

```python
import math

import jax
import jax.numpy as jnp
from jax import lax
from jax.experimental import pallas as pl
from jax.experimental.pallas import tpu as pltpu
from jax.sharding import PartitionSpec as P


def fourier_table(length, direction):
    positions = jnp.arange(length, dtype=jnp.int32)
    angles = (positions[:, None] * positions[None, :] % length).astype(jnp.float32) * (
        2.0 * math.pi / length
    )
    normalise = 1.0 / math.sqrt(length)
    cosine = jnp.cos(angles) * normalise
    sine_part = jnp.sin(angles) * normalise
    upper_row = jnp.stack([cosine, direction * sine_part])
    bottom = jnp.stack([-direction * sine_part, cosine])
    return jnp.stack([upper_row, bottom]).astype(jnp.bfloat16)


def general(current_estimate, observed_magnitude, object_bounds, damping_ordinal, retained_trials):
    runs_here = current_estimate.shape[0]
    rows_second = current_estimate.shape[3]
    length = current_estimate.shape[4]
    n_px = lax.axis_size("px")
    depth_rows = observed_magnitude.shape[0]
    middle = length // n_px
    single = jnp.float32
    forward_table = fourier_table(length, -1.0)
    inverse_table = fourier_table(length, 1.0)
    position = jnp.arange(length, dtype=jnp.int32)
    inside = (position[None, None, :] >= object_bounds[:, :, 0:1]) & (
        position[None, None, :] < object_bounds[:, :, 1:2]
    )
    damping_levels = 0.5 + 0.05 * (damping_ordinal.astype(single) + 1.0)
    batch_position = lax.axis_index("run")
    measured_here = jnp.transpose(observed_magnitude, (1, 0, 2)).reshape(
        length, depth_rows * length
    )

    def forward(current):
        batch_runs = current.shape[0]
        along_z = jnp.einsum(
            "riabn,ionk->roabk", current, forward_table, preferred_element_type=single
        ).astype(jnp.bfloat16)
        received = lax.all_to_all(along_z, "px", split_axis=4, concat_axis=2, tiled=True)
        along_x = jnp.einsum(
            "rixbm,ioxk->robmk", received, forward_table, preferred_element_type=single
        ).astype(jnp.bfloat16)
        along_x = along_x.reshape(batch_runs, 2, rows_second, middle * length)
        arrived = lax.all_to_all(along_x, "py", split_axis=3, concat_axis=2, tiled=True)
        return jnp.einsum("riyc,ioyl->rolc", arrived, forward_table, preferred_element_type=single)

    def inverse(target):
        batch_runs = target.shape[0]
        back_y = jnp.einsum(
            "rilc,ioly->royc", target, inverse_table, preferred_element_type=single
        ).astype(jnp.bfloat16)
        partial_value = lax.all_to_all(back_y, "py", split_axis=2, concat_axis=3, tiled=True)
        partial_value = partial_value.reshape(batch_runs, 2, rows_second, middle, length)
        back_x = jnp.einsum(
            "ribmk,iokx->roxbm", partial_value, inverse_table, preferred_element_type=single
        ).astype(jnp.bfloat16)
        returned = lax.all_to_all(back_x, "px", split_axis=2, concat_axis=4, tiled=True)
        return jnp.einsum(
            "riabk,iokz->roabz", returned, inverse_table, preferred_element_type=single
        )

    def relax_step(current, beta):
        spectrum = forward(current)
        amplitude = jnp.sqrt(spectrum[:, 0] * spectrum[:, 0] + spectrum[:, 1] * spectrum[:, 1])
        misfit = jnp.sum((amplitude - measured_here[None]) ** 2, axis=(1, 2))
        scaling = measured_here[None] / jnp.maximum(amplitude, 0.1)
        target = (spectrum * scaling[:, None]).astype(jnp.bfloat16)
        projected = inverse(target)
        weight = beta[:, None, None, None, None]
        outside_value = weight * current.astype(single) + (1.0 - 2.0 * weight) * projected
        updated = jnp.where(inside[None, None], projected, outside_value).astype(jnp.bfloat16)
        return (updated, misfit)

    beta_here = lax.dynamic_slice_in_dim(damping_levels, batch_position * runs_here, runs_here)
    iterate_next, misfit_first = relax_step(current_estimate, beta_here)
    misfit_total, energy = lax.psum(
        (misfit_first, jnp.sum(observed_magnitude * observed_magnitude)), ("px", "py")
    )
    errors_first = misfit_total / energy
    resident_keeper = lax.dynamic_slice_in_dim(retained_trials, batch_position, 1)
    owners = retained_trials // runs_here
    slot_index = retained_trials % runs_here
    picked = jnp.take(iterate_next, slot_index, axis=0)
    owned_here = owners == batch_position
    outgoing = jnp.where(owned_here[:, None, None, None, None], picked, jnp.zeros_like(picked))
    arrived = lax.all_to_all(outgoing, "run", split_axis=0, concat_axis=0, tiled=True)
    chosen_slot = lax.dynamic_slice_in_dim(arrived, resident_keeper[0] // runs_here, 1, 0)
    damping_closing = jnp.take(damping_levels, resident_keeper)
    iterate_final, misfit_last = relax_step(chosen_slot, damping_closing)
    total_last = lax.psum(misfit_last, ("px", "py"))
    return (iterate_next, iterate_final, errors_first, total_last / energy)


LANES = 128
GRANULE = 32
CHUNKS = 4
STEP = 16
F32 = jnp.float32
BF16 = jnp.bfloat16


def waves(rows, columns, length):
    angles = (rows[:, None] * columns[None, :] % length).astype(F32) * (2.0 * math.pi / length)
    normalise = 1.0 / math.sqrt(length)
    return jnp.cos(angles) * normalise, jnp.sin(angles) * normalise


def half_signs(shape, first):
    lane = lax.broadcasted_iota(jnp.int32, shape, len(shape) - 1)
    return jnp.where(lane < LANES // 2, first, -first)


def combine(products, rows, first):
    pieces = []
    sign = half_signs((rows, LANES), first)
    for at in range(products.shape[1] // LANES):
        cut = slice(at * LANES, (at + 1) * LANES)
        turned = pltpu.roll(products[rows:, cut], LANES // 2, 1)
        pieces.append(products[:rows, cut] + sign * turned)
    return pieces


def exchange_granules(low, high):
    lane = lax.broadcasted_iota(jnp.int32, low.shape, 1)
    even = (lane // GRANULE) % 2 == 0
    return (
        jnp.where(even, low, pltpu.roll(high, GRANULE, 1)),
        jnp.where(even, pltpu.roll(low, LANES - GRANULE, 1), high),
    )


def z_forward(slot, field, table, chunk, dims):
    peers, width, x_len, y_len, length = dims["peers"], dims["ychunk"], dims["x"], dims["y"], dims["n"]

    def body(slot_ref, field_ref, table_ref, *rest):
        outs, scratch = rest[:peers], rest[peers]
        rows = STEP * width
        first = field_ref[0, 0].reshape(rows, length)
        second = field_ref[0, 1].reshape(rows, length)
        result = jnp.dot(first, table_ref[0], preferred_element_type=F32)
        result = result + jnp.dot(second, table_ref[1], preferred_element_type=F32)
        for peer in range(peers):
            for at in range(STEP):
                scratch[peer, pl.ds(at, width, stride=STEP), :] = result[
                    at * width : (at + 1) * width, peer * LANES : (peer + 1) * LANES
                ]
        for peer in range(peers):
            outs[peer][...] = scratch[peer].reshape(width, STEP, LANES).astype(BF16)

    return pl.pallas_call(
        body,
        grid_spec=pltpu.PrefetchScalarGridSpec(
            num_scalar_prefetch=1,
            grid=(x_len // STEP,),
            in_specs=[
                pl.BlockSpec((1, 2, STEP, width, length), lambda g, s: (s[0], 0, g, chunk, 0)),
                pl.BlockSpec((2, length, 2 * length), lambda g, s: (0, 0, 0)),
            ],
            out_specs=[pl.BlockSpec((width, STEP, LANES), lambda g, s: (0, g, 0))] * peers,
            scratch_shapes=[pltpu.VMEM((peers, width * STEP, LANES), F32)],
        ),
        out_shape=[jax.ShapeDtypeStruct((width, x_len, LANES), BF16)] * peers,
        name="z_forward",
    )(slot, field, table)


def x_forward(parts, table, dims):
    peers, width, x_len, length = dims["peers"], dims["ychunk"], dims["x"], dims["n"]
    half = length // 2

    def body(*refs):
        ins, table_ref, outs, scratch = refs[:peers], refs[peers], refs[peers + 1 : peers + 3], refs[peers + 3]

        def one_pair(at, carry):
            columns = []
            for inner in range(2):
                columns.append(jnp.concatenate([ref[2 * at + inner] for ref in ins], axis=0))
            data = jnp.concatenate(columns, axis=1)
            products = jnp.dot(table_ref[...], data, preferred_element_type=F32)
            for inner, piece in enumerate(combine(products, length, 1.0)):
                kept, sent = exchange_granules(piece[:half], piece[half:])
                scratch[0, pl.ds(2 * at + inner, half, stride=STEP), :] = kept
                scratch[1, pl.ds(2 * at + inner, half, stride=STEP), :] = sent
            return carry

        lax.fori_loop(0, STEP // 2, one_pair, 0)
        for side in range(2):
            outs[side][...] = scratch[side].reshape(half, STEP, LANES).astype(BF16)

    return pl.pallas_call(
        body,
        grid=(width // STEP,),
        in_specs=[pl.BlockSpec((STEP, x_len, LANES), lambda g: (g, 0, 0))] * peers
        + [pl.BlockSpec((2 * length, length), lambda g: (0, 0))],
        out_specs=[pl.BlockSpec((half, STEP, LANES), lambda g: (0, g, 0))] * 2,
        out_shape=[jax.ShapeDtypeStruct((half, width, LANES), BF16)] * 2,
        scratch_shapes=[pltpu.VMEM((2, half * STEP, LANES), F32)],
        name="x_forward",
    )(*parts, table)


def y_both(parts, measured, table, inverse_table, chunk, dims):
    count, width, y_len, length, kchunk = len(parts), dims["ychunk"], dims["y"], dims["n"], dims["kchunk"]
    steps = kchunk // STEP

    def body(*refs):
        ins = refs[:count]
        measured_ref, table_ref, inverse_ref = refs[count : count + 3]
        outs = refs[count + 3 : count + 5]
        misfit_ref, scratch = refs[count + 5 :]

        @pl.when(pl.program_id(0) == 0)
        def _():
            misfit_ref[...] = jnp.zeros_like(misfit_ref)

        def one_pair(at, total):
            columns = []
            for inner in range(2):
                columns.append(jnp.concatenate([ref[2 * at + inner] for ref in ins], axis=0))
            data = jnp.concatenate(columns, axis=1)
            products = jnp.dot(table_ref[...], data, preferred_element_type=F32)
            targets = []
            for inner, spectrum in enumerate(combine(products, length, 1.0)):
                square = spectrum * spectrum
                amplitude = jnp.sqrt(square + pltpu.roll(square, LANES // 2, 1))
                magnitude = measured_ref[2 * at + inner]
                gap = amplitude - magnitude
                total = total + jnp.sum((gap * gap).reshape(length // 8, 8, LANES), axis=0)
                scaling = magnitude / jnp.maximum(amplitude, 0.1)
                targets.append((spectrum * scaling).astype(BF16))
            back = jnp.dot(inverse_ref[...], jnp.concatenate(targets, axis=1), preferred_element_type=F32)
            for inner, piece in enumerate(combine(back, length, -1.0)):
                scratch[0, pl.ds(2 * at + inner, y_len, stride=STEP), :] = piece[:y_len]
                scratch[1, pl.ds(2 * at + inner, y_len, stride=STEP), :] = piece[y_len:]
            return total

        total = lax.fori_loop(0, STEP // 2, one_pair, jnp.zeros((8, LANES), F32))
        misfit_ref[...] += total
        for side in range(2):
            outs[side][...] = scratch[side].reshape(y_len, STEP, LANES).astype(BF16)

    base = chunk * steps
    return pl.pallas_call(
        body,
        grid=(steps,),
        in_specs=[pl.BlockSpec((STEP, width, LANES), lambda g: (base + g, 0, 0))] * count
        + [
            pl.BlockSpec((STEP, length, LANES), lambda g: (base + g, 0, 0)),
            pl.BlockSpec((2 * length, length), lambda g: (0, 0)),
            pl.BlockSpec((2 * length, length), lambda g: (0, 0)),
        ],
        out_specs=[pl.BlockSpec((y_len, STEP, LANES), lambda g: (0, g, 0))] * 2
        + [pl.BlockSpec((8, LANES), lambda g: (0, 0))],
        out_shape=[jax.ShapeDtypeStruct((y_len, kchunk, LANES), BF16)] * 2
        + [jax.ShapeDtypeStruct((8, LANES), F32)],
        scratch_shapes=[pltpu.VMEM((2, y_len * STEP, LANES), F32)],
        name="y_both",
    )(*parts, measured, table, inverse_table)


def x_inverse(own, other, table, chunk, dims):
    count, peers, width, x_len, length = len(own), dims["peers"], dims["ychunk"], dims["x"], dims["n"]
    kchunk = dims["kchunk"]
    steps = width // STEP

    def body(*refs):
        own_refs, other_refs, table_ref = refs[:count], refs[count : 2 * count], refs[2 * count]
        outs, scratch = refs[2 * count + 1 : 2 * count + 1 + peers], refs[2 * count + 1 + peers]

        def one_pair(at, carry):
            columns = []
            for inner in range(2):
                near = jnp.concatenate([ref[2 * at + inner] for ref in own_refs], axis=0).astype(F32)
                far = jnp.concatenate([ref[2 * at + inner] for ref in other_refs], axis=0).astype(F32)
                low, high = exchange_granules(near, far)
                columns.append(jnp.concatenate([low, high], axis=0).astype(BF16))
            data = jnp.concatenate(columns, axis=1)
            products = jnp.dot(table_ref[...], data, preferred_element_type=F32)
            for inner, piece in enumerate(combine(products, length, -1.0)):
                for peer in range(peers):
                    scratch[peer, pl.ds(2 * at + inner, x_len, stride=STEP), :] = piece[
                        peer * x_len : (peer + 1) * x_len
                    ]
            return carry

        lax.fori_loop(0, STEP // 2, one_pair, 0)
        for peer in range(peers):
            outs[peer][...] = scratch[peer].reshape(x_len, STEP, LANES).astype(BF16)

    base = chunk * steps
    return pl.pallas_call(
        body,
        grid=(steps,),
        in_specs=[pl.BlockSpec((STEP, kchunk, LANES), lambda g: (base + g, 0, 0))] * (2 * count)
        + [pl.BlockSpec((2 * length, length), lambda g: (0, 0))],
        out_specs=[pl.BlockSpec((x_len, STEP, LANES), lambda g: (0, g, 0))] * peers,
        out_shape=[jax.ShapeDtypeStruct((x_len, width, LANES), BF16)] * peers,
        scratch_shapes=[pltpu.VMEM((peers, x_len * STEP, LANES), F32)],
        name="x_inverse",
    )(*own, *other, table)


def z_inverse(slot, beta, parts, field, field_chunk, bounds, table, buffer, chunk, keep, dims):
    peers, width, x_len, y_len, length = dims["peers"], dims["ychunk"], dims["x"], dims["y"], dims["n"]
    runs = dims["runs"] if keep else 1
    aliased = buffer is not None

    def body(slot_ref, beta_ref, *refs):
        ins, (field_ref, bounds_ref, table_ref) = refs[:peers], refs[peers : peers + 3]
        outs = refs[peers + 3 + aliased :]
        rows = STEP * width
        data = jnp.concatenate([ref[...].reshape(rows, LANES) for ref in ins], axis=1)
        result = jnp.dot(data, table_ref[...], preferred_element_type=F32)
        lower = bounds_ref[:, :, 0:1].reshape(rows, 1)
        upper = bounds_ref[:, :, 1:2].reshape(rows, 1)
        position = lax.broadcasted_iota(jnp.int32, (rows, length), 1)
        inside = (position >= lower) & (position < upper)
        weight = beta_ref[0]
        for part in range(2):
            projected = result[:, part * length : (part + 1) * length]
            current = field_ref[0, part].reshape(rows, length).astype(F32)
            outside = weight * current + (1.0 - 2.0 * weight) * projected
            updated = jnp.where(inside, projected, outside).astype(BF16).reshape(STEP, width, length)
            outs[0][0, part] = updated
            if keep:
                outs[1][0, part] = updated

    block = (1, 2, STEP, width, length)
    in_specs = [pl.BlockSpec((STEP, width, LANES), lambda g, s, b: (g, 0, 0))] * peers + [
        pl.BlockSpec(block, lambda g, s, b: (s[0], 0, g, field_chunk, 0)),
        pl.BlockSpec((STEP, width, 2), lambda g, s, b: (g, chunk, 0)),
        pl.BlockSpec((2 * length, 2 * length), lambda g, s, b: (0, 0)),
    ]
    operands = list(parts) + [field, bounds, table]
    out_specs = [pl.BlockSpec(block, lambda g, s, b: (s[0], 0, g, chunk, 0))]
    out_shape = [jax.ShapeDtypeStruct((runs, 2, x_len, y_len, length), BF16)]
    if keep:
        out_specs.append(pl.BlockSpec(block, lambda g, s, b: (0, 0, g, 0, 0)))
        out_shape.append(jax.ShapeDtypeStruct((1, 2, x_len, width, length), BF16))
    aliases = {}
    if aliased:
        in_specs.append(pl.BlockSpec(memory_space=pl.ANY))
        operands.append(buffer)
        aliases = {2 + len(operands) - 1: 0}
    return pl.pallas_call(
        body,
        grid_spec=pltpu.PrefetchScalarGridSpec(
            num_scalar_prefetch=2, grid=(x_len // STEP,), in_specs=in_specs, out_specs=out_specs
        ),
        out_shape=out_shape,
        input_output_aliases=aliases,
        name="z_inverse",
    )(slot, beta, *operands)


def pick(index, choices):
    result = choices[0]
    for at in range(1, len(choices)):
        result = jnp.where(index == at, choices[at], result)
    return result


def pipelined(current_estimate, observed_magnitude, object_bounds, damping_ordinal, retained_trials):
    runs_here, _, x_len, y_len, length = current_estimate.shape
    peers = lax.axis_size("px")
    me_x, me_y, plane = lax.axis_index("px"), lax.axis_index("py"), lax.axis_index("run")
    half, middle = length // 2, length // peers
    dims = {
        "peers": peers, "x": x_len, "y": y_len, "n": length, "runs": runs_here,
        "ychunk": y_len // CHUNKS, "kchunk": half // CHUNKS,
    }
    whole = jnp.arange(length, dtype=jnp.int32)
    mine_k2 = (me_x ^ (whole // middle)) * middle + (me_y ^ (whole % middle // GRANULE)) * GRANULE + whole % GRANULE
    mine_x = (me_x ^ (whole // x_len)) * x_len + whole % x_len
    mine_y = (me_y ^ (whole // y_len)) * y_len + whole % y_len

    cosine, sine = waves(whole, mine_k2, length)
    cosine, sine = (part.reshape(length, peers, middle) for part in (cosine, sine))
    table_z = jnp.stack([
        jnp.stack([cosine, -sine], axis=2).reshape(length, 2 * length),
        jnp.stack([sine, cosine], axis=2).reshape(length, 2 * length),
    ]).astype(BF16)
    cosine, sine = waves(mine_k2, whole, length)
    upper = jnp.concatenate([cosine, sine], axis=1).reshape(peers, middle, 2 * length)
    lower = jnp.concatenate([-sine, cosine], axis=1).reshape(peers, middle, 2 * length)
    table_z_back = jnp.stack([upper, lower], axis=1).reshape(2 * length, 2 * length).astype(BF16)
    table_x = jnp.concatenate(waves(whole, mine_x, length), axis=0).astype(BF16)
    table_x_back = jnp.concatenate(waves(mine_x, whole, length), axis=0).astype(BF16)
    table_y = jnp.concatenate(waves(whole, mine_y, length), axis=0).astype(BF16)
    table_y_back = jnp.concatenate(waves(mine_y, whole, length), axis=0).astype(BF16)

    measured = observed_magnitude.reshape(GRANULE, length, 2, half)
    measured = jnp.transpose(measured, (3, 1, 2, 0)).reshape(half, length, 2 * GRANULE)
    measured = jnp.concatenate([measured, measured], axis=2)

    swap_x = {turn: [(at, at ^ turn) for at in range(peers)] for turn in range(1, peers)}
    swap_y = [(0, 1), (1, 0)]

    def across_x(parts):
        return [parts[0]] + [lax.ppermute(parts[turn], "px", swap_x[turn]) for turn in range(1, peers)]

    def forward(slot, fields, chunk_of):
        kept, received = [], []
        for chunk in range(CHUNKS):
            field, at = fields[chunk], chunk_of(chunk)
            parts = across_x(z_forward(slot, field, table_z, at, dims))
            near, far = x_forward(parts, table_x, dims)
            kept.append(near)
            received.append(lax.ppermute(far, "py", swap_y))
        return kept + received

    def middle_pass(parts):
        own, other, misfit = [], [], []
        for chunk in range(CHUNKS):
            near, far, part = y_both(parts, measured, table_y, table_y_back, chunk, dims)
            own.append(near)
            other.append(lax.ppermute(far, "py", swap_y))
            misfit.append(part)
        return own, other, 0.5 * jnp.sum(sum(misfit))

    def inverse(slot, beta, own, other, fields, chunk_of, buffer, keep):
        copies = []
        for chunk in range(CHUNKS):
            parts = across_x(x_inverse(own, other, table_x_back, chunk, dims))
            done = z_inverse(
                slot, beta, parts, fields[chunk], chunk_of(chunk), object_bounds, table_z_back,
                buffer, chunk, keep, dims,
            )
            buffer = done[0]
            if keep:
                copies.append(done[1])
        return buffer, copies

    damping_levels = 0.5 + 0.05 * (damping_ordinal.astype(F32) + 1.0)
    trial = jnp.arange(retained_trials.shape[0], dtype=jnp.int32)

    def destination(run):
        hit = retained_trials == run
        return jnp.where(jnp.any(hit), jnp.sum(jnp.where(hit, trial, 0)), -1)

    def order(at):
        first = jnp.where((destination(2 * at) < 0) & (destination(2 * at + 1) >= 0), 1, 0)
        return first, destination(2 * at + first), destination(2 * at + 1 - first)

    lead, lead_to, trail_to = order(plane)
    slots = [lead.astype(jnp.int32).reshape(1), (1 - lead).astype(jnp.int32).reshape(1)]
    betas = [lax.dynamic_slice_in_dim(damping_levels, plane * runs_here + slot[0], 1) for slot in slots]
    source = [current_estimate] * CHUNKS

    spread = [forward(slot, source, lambda chunk: chunk) for slot in slots]
    turned = [middle_pass(parts) for parts in spread]
    buffer, copies = None, []
    for slot, beta, (own, other, _) in zip(slots, betas, turned):
        buffer, copy = inverse(slot, beta, own, other, source, lambda chunk: chunk, buffer, True)
        copies.append(copy)

    inner = (plane == 1) | (plane == 2)
    near_edge = jnp.where(plane <= 1, 0, 3)
    _, edge_lead_to, edge_trail_to = order(near_edge)
    from_edge_lead = jnp.where(inner, edge_lead_to, -1)
    from_edge_trail = jnp.where(inner, edge_trail_to, -1)
    mirror_plane = 3 - plane
    _, mirror_lead_to, mirror_trail_to = order(mirror_plane)

    def crossing(at, lead_at, edge_lead_at, trail_at, edge_trail_at):
        low = at <= 1
        wants = [(to >= 0) & ((to <= 1) != low) for to in (lead_at, edge_lead_at, trail_at, edge_trail_at)]
        lane_one = jnp.where(wants[0], 0, jnp.where(wants[1], 1, -1))
        second = -1
        for index in (3, 2, 1):
            second = jnp.where(wants[index] & (lane_one != index), index, second)
        return lane_one.astype(jnp.int32), jnp.asarray(second, jnp.int32)

    lane_one, lane_two = crossing(plane, lead_to, from_edge_lead, trail_to, from_edge_trail)
    far_edge = jnp.where(plane <= 1, 3, 0)
    _, far_edge_lead_to, far_edge_trail_to = order(far_edge)
    mirror_to = [mirror_lead_to, far_edge_lead_to, mirror_trail_to, far_edge_trail_to]
    mirror_one, mirror_two = crossing(mirror_plane, *mirror_to)

    def chosen_to(index):
        result = -1
        for at in range(4):
            result = jnp.where(index == at, mirror_to[at], result)
        return jnp.where(inner, result, -1)

    over_one_to, over_two_to = chosen_to(mirror_one), chosen_to(mirror_two)
    outer = jnp.where(plane <= 1, 0, 3)
    out_from = [lead_to, trail_to, over_one_to, over_two_to]
    out_index = jnp.int32(0)
    for at in range(4):
        out_index = jnp.where(out_from[at] == outer, at, out_index)
    arrivals = [lead_to, trail_to, from_edge_lead, from_edge_trail, over_one_to, over_two_to]
    final_index = jnp.int32(6)
    for at in range(6):
        final_index = jnp.where(arrivals[at] == plane, at, final_index)

    inward, across, outward = [(0, 1), (3, 2)], [(1, 2), (2, 1)], [(1, 0), (2, 3)]
    moved = []
    for chunk in range(CHUNKS):
        first, second = copies[0][chunk], copies[1][chunk]
        edge_first = lax.ppermute(first, "run", inward)
        edge_second = lax.ppermute(second, "run", inward)
        over_one = lax.ppermute(jnp.where(lane_one == 1, edge_first, first), "run", across)
        over_two = lax.ppermute(pick(lane_two, [edge_first, edge_first, second, edge_second]), "run", across)
        out = lax.ppermute(pick(out_index, [first, second, over_one, over_two]), "run", outward)
        moved.append(pick(final_index, [first, second, edge_first, edge_second, over_one, over_two, out]))

    keeper = lax.dynamic_slice_in_dim(retained_trials, plane, 1)
    beta_closing = lax.dynamic_slice_in_dim(damping_levels, keeper[0], 1)
    only = jnp.zeros((1,), jnp.int32)
    own, other, misfit_last = middle_pass(forward(only, moved, lambda chunk: 0))
    iterate_final, _ = inverse(only, beta_closing, own, other, moved, lambda chunk: 0, None, False)

    energy = jnp.sum(observed_magnitude * observed_magnitude)
    sums = lax.psum(jnp.stack([turned[0][2], turned[1][2], misfit_last, energy]), ("px", "py"))
    errors = sums[:3] / sums[3]
    errors_first = jnp.where(lead == 0, errors[:2], errors[1::-1])
    return (buffer, iterate_final, errors_first, errors[2:])


def solution(mesh):
    sizes = dict(mesh.shape)
    fits = sizes["px"] == 4 and sizes["py"] == 2 and sizes["run"] == 4
    return jax.shard_map(
        pipelined if fits else general,
        mesh=mesh,
        in_specs=(
            P("run", None, "px", "py", None),
            P(("px", "py"), None, None),
            P("px", "py", None),
            P(),
            P(),
        ),
        out_specs=(
            P("run", None, "px", "py", None),
            P("run", None, "px", "py", None),
            P("run"),
            P("run"),
        ),
        check_vma=False,
    )
```
